1024 devices in a mesh: row: 32 (over z), col: 16 (over y, x), layer: 2 (over core).
Axes of the slice: x: 4, y: 4, z: 32, core: 2. Of those that a mesh axis runs over, the one named last changes fastest.
Arguments:
- left_blocks: bfloat16 [8192, 2, 4096], P('row', 'layer', 'col'), may hold values from 4.8577785e-06 to 0.00048828125
- batch_blocks: bfloat16 [2, 4096, 8192], P('layer', 'row', 'col'), may hold values from 0.019897461 to 2
- left_mask: int32 [64, 2, 32], P('row', 'layer', 'col'), may hold values 0 or 1
- batch_mask: int32 [2, 32, 64], P('layer', 'row', 'col'), may hold values 0 or 1
- prune_mask: int32 [64, 64], P('row', ('col', 'layer')), may hold values 0 or 1
Outputs:
- normalized: float32 [8192, 8192], P('row', ('col', 'layer'))
The draws below stay inside these ranges and needn't reach their ends.
All inputs are finite; a program needn't handle non-finite values. No bound on the sum of `left_mask` or of `batch_mask` or of `prune_mask` on one device may be relied on, other than what follows from the above.
Results may differ from the reference program's by a relative error of at most 0.0003.
Values may be sent and summed in bfloat16 or wider, within the bound.
A program may use at most 32 MiB of HBM per device.

```python
import math
import jax
import jax.numpy as jnp

M = 8192
KH = 4096
NB = 8192
MT = 64
KT = 32
NBT = 64


def with_ends(values, own_key, low, high):
    spot = [jax.random.randint(jax.random.fold_in(own_key, axis), (), 0, length) for axis, length in enumerate(values.shape)]
    longest = values.shape.index(max(values.shape))
    next_to = spot[:longest] + [(spot[longest] + 1) % values.shape[longest]] + spot[longest + 1:]
    return values.at[tuple(spot)].set(low).at[tuple(next_to)].set(high)


def level_of(rng, dims, split, smallest, high):
    loudness, own = 1.0, jax.random.fold_in(rng, 6)
    for axis_at, shards_of in split:
        heights = jnp.exp(jax.random.uniform(jax.random.fold_in(own, axis_at), (shards_of,), jnp.float32, smallest / len(split), high / len(split)))
        loudness = loudness * jnp.repeat(heights, dims[axis_at] // shards_of).reshape([-1 if axis == axis_at else 1 for axis in range(len(dims))])
    return loudness


def setup_inputs(seed: int = 0) -> dict:
    arg_keys = jax.random.split(jax.random.key(seed), 6)
    left_blocks = jnp.clip(jnp.exp(math.log(0.00048828125) - 4.61031033 * jax.random.uniform(arg_keys[0], (M, 2, KH), jnp.float32) ** level_of(arg_keys[0], (M, 2, KH), ((0, 32), (1, 2), (2, 16)), -0.2, 0.2)), 4.857778549194336e-06, 0.00048828125).astype(jnp.bfloat16)
    batch_blocks = jnp.clip(jnp.exp(math.log(2.0) - 4.61031033 * jax.random.uniform(arg_keys[1], (2, KH, NB), jnp.float32) ** level_of(arg_keys[1], (2, KH, NB), ((0, 2), (1, 32), (2, 16)), -0.2, 0.2)), 0.019897461, 2.0).astype(jnp.bfloat16)
    left_mask = with_ends((jax.random.randint(arg_keys[2], (MT, 2, KT), 0, 4) < 3).astype(jnp.int32), jax.random.fold_in(arg_keys[2], 1), 0, 1)
    batch_mask = with_ends((jax.random.randint(arg_keys[3], (2, KT, NBT), 0, 4) < 3).astype(jnp.int32), jax.random.fold_in(arg_keys[3], 1), 0, 1)
    prune_mask = with_ends((jax.random.randint(arg_keys[4], (MT, NBT), 0, 3) < 2).astype(jnp.int32), jax.random.fold_in(arg_keys[4], 1), 0, 1)
    return {"left_blocks": left_blocks, "batch_blocks": batch_blocks, "left_mask": left_mask, "batch_mask": batch_mask, "prune_mask": prune_mask}


def widen_left(mask, tile_size):
    first, middle, last = mask.shape
    spread = jnp.broadcast_to(mask.astype(jnp.bfloat16)[:, None, :, :, None], (first, tile_size, middle, last, tile_size))
    return spread.reshape(first * tile_size, middle, last * tile_size)


def widen_right(mask, tile_size):
    first, middle, last = mask.shape
    spread = jnp.broadcast_to(mask.astype(jnp.bfloat16)[:, :, None, :, None], (first, middle, tile_size, last, tile_size))
    return spread.reshape(first, middle * tile_size, last * tile_size)


def widen_pair(mask, tile_size):
    first, last = mask.shape
    spread = jnp.broadcast_to(mask.astype(jnp.float32)[:, None, :, None], (first, tile_size, last, tile_size))
    return spread.reshape(first * tile_size, last * tile_size)


def reference(left_blocks, batch_blocks, left_mask, batch_mask, prune_mask):
    tile_size = left_blocks.shape[0] // left_mask.shape[0]
    left = (left_blocks * widen_left(left_mask, tile_size)).astype(jnp.bfloat16)
    right = (batch_blocks * widen_right(batch_mask, tile_size)).astype(jnp.bfloat16)
    product = jnp.dot(left[:, 0, :], right[0], preferred_element_type=jnp.float32)
    product = product + jnp.dot(left[:, 1, :], right[1], preferred_element_type=jnp.float32)
    inflated = product * product * widen_pair(prune_mask, tile_size)
    col_sums = jnp.sum(inflated, axis=0)
    return inflated * (M / (col_sums + 1e-6))
```

```python
import functools

import jax
import jax.numpy as jnp
from jax import lax
from jax.experimental import pallas as pl
from jax.experimental.pallas import tpu as pltpu
from jax.sharding import PartitionSpec as P

epsilon = 1e-06
MESH = pl.DeviceIdType.MESH
SIDE = 4


def kernel(
    nz,
    left_ref,
    right_ref,
    left_mask,
    right_mask,
    prune_mask,
    out_ref,
    left_in,
    right_in,
    left_all,
    right_all,
    right_swap,
    acc,
    own_sum,
    near_sums,
    window_sum,
    far_sums,
    in_sem,
    swap_sem,
    ring_send,
    ring_recv,
    first_send,
    first_recv,
    second_send,
    second_recv,
    pass_sem,
    near_send,
    near_recv,
    far_send,
    far_recv,
):
    r = lax.axis_index("row")
    c = lax.axis_index("col")
    l = lax.axis_index("layer")
    other = 1 - l
    y, x = c // SIDE, c % SIDE

    def at_z(step):
        return (lax.rem(r + step + nz, nz), c, l)

    def at_x(step):
        return (r, y * SIDE + lax.rem(x + step, SIDE), l)

    def at_y(step):
        return (r, lax.rem(y + step, SIDE) * SIDE + x, l)

    partner = (r, c, other)

    take_left = pltpu.make_async_copy(left_ref, left_in, in_sem.at[0])
    take_right = pltpu.make_async_copy(right_ref, right_in, in_sem.at[1])
    take_right.start()
    take_left.start()

    barrier = pltpu.get_barrier_semaphore()
    greeted = [at_z(1), at_z(-1), partner]
    for step in range(1, SIDE):
        greeted += [at_x(step), at_y(step)]
    for device in greeted:
        pl.semaphore_signal(barrier, inc=1, device_id=device, device_id_type=MESH)

    tile = left_in.shape[1] // 2
    half = right_in.shape[1] // 2
    take_right.wait()
    for part in range(half // tile):
        mask = right_mask[0, 0, 2 * l + part].astype(jnp.float32)
        block = right_in[:, pl.ds(pl.multiple_of(l * half + part * tile, tile), tile)]
        right_all[l, r, :, part * tile : (part + 1) * tile] = (block.astype(jnp.float32) * mask).astype(jnp.bfloat16)
        mask = right_mask[0, 0, 2 * other + part].astype(jnp.float32)
        block = right_in[:, pl.ds(pl.multiple_of(other * half + part * tile, tile), tile)]
        right_swap[:, part * tile : (part + 1) * tile] = (block.astype(jnp.float32) * mask).astype(jnp.bfloat16)
    take_left.wait()
    for tall in range(2):
        for wide in range(2):
            mask = left_mask[tall, 0, wide].astype(jnp.float32)
            block = left_in[tall * tile : (tall + 1) * tile, wide * tile : (wide + 1) * tile]
            left_all[l, 2 * c + wide, tall * tile : (tall + 1) * tile, :] = (block.astype(jnp.float32) * mask).astype(
                jnp.bfloat16
            )
    acc[...] = jnp.zeros_like(acc)
    pl.semaphore_wait(barrier, len(greeted))

    hops = ((nz // 2, nz // 2 - 1), (nz // 2 - 1, nz // 2))
    slices = (l, other)
    ways = (1, -1)

    def origin(way, step):
        return lax.rem(r - ways[way] * (step + 1) + 2 * nz, nz)

    def ring_copy(way, kind, step):
        block = right_all.at[slices[kind], origin(way, step - 1)]
        return pltpu.make_async_remote_copy(
            src_ref=block,
            dst_ref=block,
            send_sem=ring_send.at[way, kind, step],
            recv_sem=ring_recv.at[way, kind, step],
            device_id=at_z(ways[way]),
            device_id_type=MESH,
        )

    def ring_arrived(way, kind, step):
        block = right_all.at[slices[kind], origin(way, step)]
        pltpu.make_async_remote_copy(
            src_ref=block,
            dst_ref=block,
            send_sem=ring_send.at[way, kind, step],
            recv_sem=ring_recv.at[way, kind, step],
            device_id=at_z(ways[way]),
            device_id_type=MESH,
        ).wait_recv()

    swap = pltpu.make_async_remote_copy(
        src_ref=right_swap,
        dst_ref=right_all.at[l, r],
        send_sem=swap_sem.at[0],
        recv_sem=swap_sem.at[1],
        device_id=partner,
        device_id_type=MESH,
    )
    swap.start()
    for way in range(2):
        ring_copy(way, 0, 0).start()

    peers = (at_x, at_y)

    def piece(way, back):
        if way == 0:
            return 2 * (y * SIDE + lax.rem(x + SIDE - back, SIDE))
        return 2 * (lax.rem(y + SIDE - back, SIDE) * SIDE + x) + 1

    def first_copy(way, step, place):
        block = left_all.at[l, place]
        return pltpu.make_async_remote_copy(
            src_ref=block,
            dst_ref=block,
            send_sem=first_send.at[way, step - 1],
            recv_sem=first_recv.at[way, step - 1],
            device_id=peers[way](step),
            device_id_type=MESH,
        )

    def second_copy(way, back, step, place):
        block = left_all.at[l, place]
        return pltpu.make_async_remote_copy(
            src_ref=block,
            dst_ref=block,
            send_sem=second_send.at[way, back, step - 1],
            recv_sem=second_recv.at[way, back, step - 1],
            device_id=peers[1 - way](step),
            device_id_type=MESH,
        )

    def far_place(way, back, step):
        if way == 0:
            return 2 * (lax.rem(y + SIDE - step, SIDE) * SIDE + lax.rem(x + SIDE - back, SIDE))
        return 2 * (lax.rem(y + SIDE - back, SIDE) * SIDE + lax.rem(x + SIDE - step, SIDE)) + 1

    for step in range(1, SIDE):
        for way in range(2):
            first_copy(way, step, piece(way, 0)).start()
    for step in range(1, SIDE):
        for way in range(2):
            second_copy(way, 0, step, piece(way, 0)).start()

    swap.wait_recv()
    for way in range(2):
        ring_copy(way, 1, 0).start()

    def ring_step(step, last=0):
        for kind in range(2):
            for way in range(2):
                if last and step >= hops[way][kind]:
                    continue
                ring_arrived(way, kind, step)
                if not last or step + 1 < hops[way][kind]:
                    ring_copy(way, kind, step + 1).start()

    def multiply(kind, row):
        acc[...] += jnp.dot(
            left_all[slices[kind], row], right_all[slices[kind], row], preferred_element_type=jnp.float32
        )

    def multiply_step(step):
        for way in range(2):
            for kind in range(2):
                multiply(kind, origin(way, step))

    ring_step(0)
    ring_step(1)
    for back in range(1, SIDE):
        for way in range(2):
            first_copy(way, back, piece(way, back)).wait_recv()
            for step in range(1, SIDE):
                second_copy(way, back, step, piece(way, back)).start()
    middle = nz // 4
    lax.fori_loop(2, middle, lambda step, _: (ring_step(step), None)[1], None)
    for step in range(1, SIDE):
        for back in range(SIDE):
            for way in range(2):
                second_copy(way, back, step, far_place(way, back, step)).wait_recv()
    hand_over = pltpu.make_async_remote_copy(
        src_ref=left_all.at[l],
        dst_ref=left_all.at[l],
        send_sem=pass_sem.at[0],
        recv_sem=pass_sem.at[1],
        device_id=partner,
        device_id_type=MESH,
    )
    hand_over.start()
    ring_step(middle)
    ring_step(middle + 1)
    pltpu.make_async_remote_copy(
        src_ref=left_all.at[other],
        dst_ref=left_all.at[other],
        send_sem=pass_sem.at[0],
        recv_sem=pass_sem.at[1],
        device_id=partner,
        device_id_type=MESH,
    ).wait_recv()
    for kind in range(2):
        multiply(kind, r)
    begin = middle + 2
    end = nz // 2 - 2
    each = begin // (end - begin) + 1

    def both(step, _):
        ring_step(step)
        for turn in range(each):
            multiply_step(each * (step - begin) + turn)

    lax.fori_loop(begin, end, both, None)
    done = each * (end - begin)
    ring_step(end, last=1)
    for step in range(done, end + 1):
        multiply_step(step)
    ring_step(end + 1, last=1)
    multiply(0, origin(0, end + 1))
    multiply(1, origin(1, end + 1))

    rows, columns = acc.shape
    for tall in range(2):
        for wide in range(2):
            span = (slice(tall * tile, (tall + 1) * tile), slice(wide * tile, (wide + 1) * tile))
            value = acc[span]
            acc[span] = value * value * prune_mask[tall, wide].astype(jnp.float32)
    own_sum[0] = jnp.sum(acc[...], axis=0, keepdims=True)

    window = nz // 4
    near = [step for step in range(-(window // 2 - 1), window // 2 + 1) if step]

    def near_copy(index, step):
        return pltpu.make_async_remote_copy(
            src_ref=own_sum.at[0],
            dst_ref=near_sums.at[index],
            send_sem=near_send.at[index],
            recv_sem=near_recv.at[index],
            device_id=at_z(step),
            device_id_type=MESH,
        )

    for index, step in sorted(enumerate(near), key=lambda pair: -abs(pair[1])):
        near_copy(index, step).start()
    total = own_sum[0]
    for index, step in enumerate(near):
        near_copy(index, step).wait_recv()
    for index in range(len(near)):
        total += near_sums[index]
    window_sum[0] = total
    far = (window // 2, -(window // 2), window // 2 + window, -(window // 2 + window))

    def far_copy(index, step):
        return pltpu.make_async_remote_copy(
            src_ref=window_sum.at[0],
            dst_ref=far_sums.at[index],
            send_sem=far_send.at[index],
            recv_sem=far_recv.at[index],
            device_id=at_z(step),
            device_id_type=MESH,
        )

    for index, step in reversed(list(enumerate(far))):
        far_copy(index, step).start()

    swap.wait_send()
    hand_over.wait_send()
    for way in range(2):
        for step in range(1, SIDE):
            first_copy(way, step, piece(way, 0)).wait_send()
            for back in range(SIDE):
                second_copy(way, back, step, piece(way, back)).wait_send()

    def ring_left(step, _):
        for way in range(2):
            for kind in range(2):
                ring_copy(way, kind, step).wait_send()

    lax.fori_loop(0, nz // 2 - 1, ring_left, None)
    ring_copy(0, 0, nz // 2 - 1).wait_send()
    ring_copy(1, 1, nz // 2 - 1).wait_send()
    for index, step in enumerate(near):
        near_copy(index, step).wait_send()

    for index, step in enumerate(far):
        far_copy(index, step).wait_recv()
    total = far_sums[0]
    for index in range(1, len(far)):
        total += far_sums[index]
    out_ref[...] = acc[...] * ((rows * nz) / (total + epsilon))
    for index, step in enumerate(far):
        far_copy(index, step).wait_send()


def on_device(nz, left_blocks, batch_blocks, left_mask, batch_mask, prune_mask):
    rows, _, depth = left_blocks.shape
    _, inner, columns = batch_blocks.shape
    tile = rows // left_mask.shape[0]
    half = columns // 2
    left = left_blocks.reshape(rows, depth)
    right = batch_blocks.reshape(inner, columns)
    dma = pltpu.SemaphoreType.DMA
    hbm = pl.BlockSpec(memory_space=pl.ANY)
    smem = pl.BlockSpec(memory_space=pltpu.SMEM)
    window = nz // 4
    return pl.pallas_call(
        functools.partial(kernel, nz),
        out_shape=jax.ShapeDtypeStruct((rows, half), jnp.float32),
        in_specs=[hbm, hbm, smem, smem, smem],
        out_specs=pl.BlockSpec(memory_space=pltpu.VMEM),
        scratch_shapes=[
            pltpu.VMEM((rows, depth), jnp.bfloat16),
            pltpu.VMEM((inner, columns), jnp.bfloat16),
            pltpu.VMEM((2, 2 * SIDE * SIDE, rows, tile), jnp.bfloat16),
            pltpu.VMEM((2, nz, inner, half), jnp.bfloat16),
            pltpu.VMEM((inner, half), jnp.bfloat16),
            pltpu.VMEM((rows, half), jnp.float32),
            pltpu.VMEM((1, 1, half), jnp.float32),
            pltpu.VMEM((window - 1, 1, half), jnp.float32),
            pltpu.VMEM((1, 1, half), jnp.float32),
            pltpu.VMEM((4, 1, half), jnp.float32),
            dma((2,)),
            dma((2,)),
            dma((2, 2, nz // 2)),
            dma((2, 2, nz // 2)),
            dma((2, SIDE - 1)),
            dma((2, SIDE - 1)),
            dma((2, SIDE, SIDE - 1)),
            dma((2, SIDE, SIDE - 1)),
            dma((2,)),
            dma((window - 1,)),
            dma((window - 1,)),
            dma((4,)),
            dma((4,)),
        ],
        compiler_params=pltpu.CompilerParams(collective_id=0, has_side_effects=True),
    )(left, right, left_mask, batch_mask, prune_mask)


def solution(mesh):
    placed = (
        P("row", "layer", "col"),
        P("layer", "row", "col"),
        P("row", "layer", "col"),
        P("layer", "row", "col"),
        P("row", ("col", "layer")),
    )
    return jax.shard_map(
        functools.partial(on_device, mesh.shape["row"]),
        mesh=mesh,
        in_specs=placed,
        out_specs=P("row", ("col", "layer")),
        check_vma=False,
    )
```

```python
import functools

import jax
import jax.numpy as jnp
from jax import lax
from jax.experimental import pallas as pl
from jax.experimental.pallas import tpu as pltpu
from jax.sharding import PartitionSpec as P

epsilon = 1e-06
MESH = pl.DeviceIdType.MESH
SIDE = 4


def kernel(
    nz,
    left_ref,
    right_ref,
    left_mask,
    right_mask,
    prune_mask,
    out_ref,
    left_in,
    right_in,
    left_all,
    right_all,
    acc,
    own_sum,
    sums,
    in_sem,
    swap_send,
    swap_recv,
    ring_send,
    ring_recv,
    pass_send,
    pass_recv,
    left_send,
    first_recv,
    second_recv,
    left_pass_send,
    left_pass_recv,
    sum_sem,
):
    r = lax.axis_index("row")
    c = lax.axis_index("col")
    l = lax.axis_index("layer")
    y, x = c // SIDE, c % SIDE
    deep = left_all.shape[3]
    tile = deep
    half = right_all.shape[3]
    slots = ring_recv.shape[2]

    def at_z(step):
        return (lax.rem(r + step + nz, nz), c, l)

    def at_x(step):
        return (r, y * SIDE + lax.rem(x + step, SIDE), l)

    def at_y(step):
        return (r, lax.rem(y + step, SIDE) * SIDE + x, l)

    partner = (r, c, 1 - l)

    def send(block, send_sem, recv_sem, device):
        return pltpu.make_async_remote_copy(
            src_ref=block,
            dst_ref=block,
            send_sem=send_sem,
            recv_sem=recv_sem,
            device_id=device,
            device_id_type=MESH,
        )

    take_right = pltpu.make_async_copy(right_ref, right_in, in_sem.at[0])
    take_left = pltpu.make_async_copy(left_ref, left_in, in_sem.at[1])
    take_right.start()
    take_left.start()

    barrier = pltpu.get_barrier_semaphore()

    def greet(devices):
        for device in devices:
            pl.semaphore_signal(barrier, inc=1, device_id=device, device_id_type=MESH)

    greet([partner])
    ring_greeted = [at_z(1), at_z(-1)]
    left_greeted = [peer(step) for step in range(1, SIDE) for peer in (at_x, at_y)]
    pl.when(l == 1)(lambda: greet(ring_greeted))
    pl.when(l == 0)(lambda: greet(left_greeted))

    own_slice = pl.ds(pl.multiple_of(l * deep, deep), deep)
    take_right.wait()
    for h in range(2):
        for part in range(half // tile):
            mask = right_mask[0, 0, h * (half // tile) + part].astype(jnp.float32)
            block = right_in[:, h * half + part * tile : h * half + (part + 1) * tile]
            right_all[r, h, own_slice, part * tile : (part + 1) * tile] = (block.astype(jnp.float32) * mask).astype(
                jnp.bfloat16
            )
    take_left.wait()
    for tall in range(2):
        for wide in range(2):
            mask = left_mask[tall, 0, wide].astype(jnp.float32)
            block = left_in[tall * tile : (tall + 1) * tile, wide * tile : (wide + 1) * tile]
            left_all[2 * c + wide, l, tall * tile : (tall + 1) * tile, :] = (block.astype(jnp.float32) * mask).astype(
                jnp.bfloat16
            )

    ways = (1, -1)

    def origin(way, step):
        return lax.rem(r - ways[way] * (step + 1) + 2 * nz, nz)

    def multiply(row, first=False):
        left = jnp.concatenate([left_all[row, 0], left_all[row, 1]], axis=1)
        product = jnp.dot(left, right_all[row, l], preferred_element_type=jnp.float32)
        acc[...] = product if first else acc[...] + product

    def multiply_step(step):
        for way in range(2):
            multiply(origin(way, step))

    right_swap_0 = send(right_all.at[r, :, pl.ds(0, deep)], swap_send.at[0], swap_recv.at[0], partner)
    right_swap_1 = send(right_all.at[r, 0, pl.ds(deep, deep)], swap_send.at[0], swap_recv.at[0], partner)
    left_swap_0 = send(left_all.at[pl.ds(2 * c, 2), 0], left_pass_send.at[0], left_pass_recv.at[0], partner)
    left_swap_1 = send(left_all.at[pl.ds(2 * c, 2), 1], swap_send.at[1], swap_recv.at[1], partner)
    steps = nz // 2

    def pass_group(step):
        if isinstance(step, int) and step >= steps - 2:
            return (steps - 2 + 3) // 4 + step - (steps - 2)
        return step // 4

    @pl.when(l == 1)
    def _():
        pl.semaphore_wait(barrier, 1 + len(ring_greeted))
        kinds = ((1, 0), (1, 1), (0, 0), (0, 1))
        hops = ((steps - 1, steps), (steps, steps - 1))

        def block(kind, row):
            s, h = kinds[kind]
            return right_all.at[row, h, pl.ds(s * deep, deep)]

        def ring_copy(way, kind, step, row):
            return send(
                block(kind, row), ring_send.at[0], ring_recv.at[way, kind, lax.rem(step, slots)], at_z(ways[way])
            )

        for kind in range(2):
            for way in range(2):
                ring_copy(way, kind, 0, r).start()
        right_swap_1.start()
        left_swap_1.start()
        right_swap_0.wait_recv()
        for kind in range(2, 4):
            for way in range(2):
                ring_copy(way, kind, 0, r).start()

        def ring_step(step, last=False):
            for kind, (s, h) in enumerate(kinds):
                for way in range(2):
                    if last and step >= hops[s][way]:
                        continue
                    row = origin(way, step)
                    ring_copy(way, kind, step, row).wait_recv()
                    if not last or step + 1 < hops[s][way]:
                        ring_copy(way, kind, step + 1, row).start()
                    if h == 0:
                        send(block(kind, row), pass_send.at[0], pass_recv.at[pass_group(step)], partner).start()

        begin = steps - 6
        end = steps - 2
        each = begin // (end - begin) + 1
        lax.fori_loop(0, begin, lambda step, _: (ring_step(step), None)[1], None)
        send(left_all.at[pl.ds(0, nz - 1)], left_pass_send.at[0], left_pass_recv.at[0], partner).wait_recv()
        multiply(r, first=True)

        def both(step, _):
            ring_step(step)
            for turn in range(each):
                multiply_step(each * (step - begin) + turn)

        lax.fori_loop(begin, end, both, None)
        ring_step(end, last=True)
        for step in range(each * (end - begin), end + 1):
            multiply_step(step)
        ring_step(end + 1, last=True)
        multiply(origin(0, end + 1))

    @pl.when(l == 0)
    def _():
        pl.semaphore_wait(barrier, 1 + len(left_greeted))
        right_swap_0.start()
        left_swap_0.start()
        left_swap_1.wait_recv()
        peers = (at_x, at_y)

        def place(way, back, step=0):
            to_x, to_y = (back, step) if way == 0 else (step, back)
            return 2 * (lax.rem(y + SIDE - to_y, SIDE) * SIDE + lax.rem(x + SIDE - to_x, SIDE)) + way

        def first_copy(way, step, chunk):
            return send(left_all.at[chunk], left_send.at[0], first_recv.at[way, step - 1], peers[way](step))

        def second_copy(way, back, step, chunk):
            return send(left_all.at[chunk], left_send.at[0], second_recv.at[way, back], peers[1 - way](step))

        def pass_on(chunk):
            send(left_all.at[chunk], left_pass_send.at[0], left_pass_recv.at[0], partner).start()

        for step in range(1, SIDE):
            for way in range(2):
                first_copy(way, step, place(way, 0)).start()
        for step in range(1, SIDE):
            for way in range(2):
                second_copy(way, 0, step, place(way, 0)).start()
        for back in (1, 3, 2):
            for way in range(2):
                chunk = place(way, back)
                first_copy(way, back, chunk).wait_recv()
                for step in range(1, SIDE):
                    second_copy(way, back, step, chunk).start()
                pass_on(chunk)
        for back in (0, 1, 3, 2):
            for way in range(2):
                three = left_all.at[pl.ds(0, SIDE - 1)]
                send(three, left_send.at[0], second_recv.at[way, back], partner).wait_recv()
                for step in range(1, SIDE):
                    pass_on(place(way, back, step))

        right_swap_1.wait_recv()
        multiply(r, first=True)

        def received(group, count):
            send(right_all.at[pl.ds(0, count)], pass_send.at[0], pass_recv.at[group], partner).wait_recv()

        begun = 0
        while begun < steps - 2:
            count = min(4, steps - 2 - begun)
            received(pass_group(begun), count)
            lax.fori_loop(begun, begun + count, lambda step, _: (multiply_step(step), None)[1], None)
            begun += count
        received(pass_group(steps - 2), 1)
        multiply_step(steps - 2)
        send(right_all.at[0, 0], pass_send.at[0], pass_recv.at[pass_group(steps - 1)], partner).wait_recv()
        multiply(origin(0, steps - 1))

    rows = acc.shape[0]
    column_sum = None
    for tall in range(2):
        parts = []
        for wide in range(2):
            span = (slice(tall * tile, (tall + 1) * tile), slice(wide * tile, (wide + 1) * tile))
            value = acc[span]
            value = value * value * prune_mask[tall, wide].astype(jnp.float32)
            acc[span] = value
            parts.append(jnp.sum(value, axis=0, keepdims=True))
        part = jnp.concatenate(parts, axis=1)
        column_sum = part if column_sum is None else column_sum + part
    own_sum[0] = column_sum

    far_first = [steps]
    for step in range(steps - 1, 0, -1):
        far_first += [step, nz - step]
    for index, step in enumerate(far_first):
        pltpu.make_async_remote_copy(
            src_ref=own_sum.at[0],
            dst_ref=sums.at[index],
            send_sem=sum_sem.at[0],
            recv_sem=sum_sem.at[1],
            device_id=at_z(step),
            device_id_type=MESH,
        ).start()

    @pl.when(l == 1)
    def _():
        right_swap_1.wait_send()
        left_swap_1.wait_send()
        send(right_all.at[pl.ds(0, nz - 1)], ring_send.at[0], ring_recv.at[0, 0, 0], partner).wait_send()
        send(right_all.at[pl.ds(0, nz - 1), 0], pass_send.at[0], pass_recv.at[0], partner).wait_send()

    @pl.when(l == 0)
    def _():
        right_swap_0.wait_send()
        send(left_all.at[pl.ds(0, nz - 2)], left_send.at[0], left_pass_recv.at[0], partner).wait_send()
        send(left_all.at[pl.ds(0, nz - 1)], left_pass_send.at[0], left_pass_recv.at[0], partner).wait_send()

    every = send(sums, sum_sem.at[0], sum_sem.at[1], partner)
    every.wait_recv()
    total = own_sum[0]
    for index in range(nz - 1):
        total += sums[index]
    out_ref[...] = acc[...] * ((rows * nz) / (total + epsilon))
    every.wait_send()


def on_device(nz, left_blocks, batch_blocks, left_mask, batch_mask, prune_mask):
    rows, _, depth = left_blocks.shape
    _, inner, columns = batch_blocks.shape
    tile = rows // left_mask.shape[0]
    half = columns // 2
    left = left_blocks.reshape(rows, depth)
    right = batch_blocks.reshape(inner, columns)
    dma = pltpu.SemaphoreType.DMA
    hbm = pl.BlockSpec(memory_space=pl.ANY)
    smem = pl.BlockSpec(memory_space=pltpu.SMEM)
    groups = (nz // 2 - 2 + 3) // 4 + 2
    return pl.pallas_call(
        functools.partial(kernel, nz),
        out_shape=pltpu.VMEM((rows, half), jnp.float32),
        in_specs=[hbm, hbm, smem, smem, smem],
        out_specs=pl.BlockSpec(memory_space=pltpu.VMEM),
        scratch_shapes=[
            pltpu.VMEM((rows, depth), jnp.bfloat16),
            pltpu.VMEM((inner, columns), jnp.bfloat16),
            pltpu.VMEM((nz, 2, rows, tile), jnp.bfloat16),
            pltpu.VMEM((nz, 2, 2 * inner, half), jnp.bfloat16),
            pltpu.VMEM((rows, half), jnp.float32),
            pltpu.VMEM((1, 1, half), jnp.float32),
            pltpu.VMEM((nz - 1, 1, half), jnp.float32),
            dma((2,)),
            dma((2,)),
            dma((2,)),
            dma((1,)),
            dma((2, 4, 4)),
            dma((1,)),
            dma((groups,)),
            dma((1,)),
            dma((2, SIDE - 1)),
            dma((2, SIDE)),
            dma((1,)),
            dma((1,)),
            dma((2,)),
        ],
        compiler_params=pltpu.CompilerParams(collective_id=0, has_side_effects=True),
    )(left, right, left_mask, batch_mask, prune_mask)


def solution(mesh):
    placed = (
        P("row", "layer", "col"),
        P("layer", "row", "col"),
        P("row", "layer", "col"),
        P("layer", "row", "col"),
        P("row", ("col", "layer")),
    )
    return jax.shard_map(
        functools.partial(on_device, mesh.shape["row"]),
        mesh=mesh,
        in_specs=placed,
        out_specs=P("row", ("col", "layer")),
        check_vma=False,
    )
```

```python
import functools

import jax
import jax.numpy as jnp
from jax import lax
from jax.experimental import pallas as pl
from jax.experimental.pallas import tpu as pltpu
from jax.sharding import PartitionSpec as P

epsilon = 1e-06
MESH = pl.DeviceIdType.MESH
SIDE = 4
PARTS = 2
SLOTS = 3
BEGIN = 9


def kernel(
    nz,
    left_ref,
    right_ref,
    left_mask_ref,
    right_mask_ref,
    prune_mask_ref,
    out_ref,
    left_in,
    right_in,
    left_mask,
    right_mask,
    prune_mask,
    left_all,
    right_all,
    acc,
    own_sum,
    sums,
    in_sem,
    swap_send,
    swap_recv,
    ring_send,
    ring_recv,
    pass_send,
    pass_recv,
    left_send,
    first_recv,
    second_recv,
    left_pass_send,
    left_pass_recv,
    sum_sem,
):
    r = lax.axis_index("row")
    c = lax.axis_index("col")
    l = lax.axis_index("layer")
    y, x = c // SIDE, c % SIDE
    deep = left_all.shape[3]
    tile = deep
    half = right_all.shape[3]

    def at_z(step):
        return (lax.rem(r + step + nz, nz), c, l)

    def at_x(step):
        return (r, y * SIDE + lax.rem(x + step, SIDE), l)

    def at_y(step):
        return (r, lax.rem(y + step, SIDE) * SIDE + x, l)

    partner = (r, c, 1 - l)

    def send(block, send_sem, recv_sem, device):
        return pltpu.make_async_remote_copy(
            src_ref=block,
            dst_ref=block,
            send_sem=send_sem,
            recv_sem=recv_sem,
            device_id=device,
            device_id_type=MESH,
        )

    barrier = pltpu.get_barrier_semaphore()

    def greet(devices):
        for device in devices:
            pl.semaphore_signal(barrier, inc=1, device_id=device, device_id_type=MESH)

    greet([partner])
    ring_greeted = [at_z(1), at_z(-1)]
    left_greeted = [peer(step) for step in range(1, SIDE) for peer in (at_x, at_y)]
    pl.when(l == 1)(lambda: greet(ring_greeted))
    pl.when(l == 0)(lambda: greet(left_greeted))

    fetches = [
        pltpu.make_async_copy(source, target, in_sem.at[index])
        for index, (source, target) in enumerate(
            (
                (right_ref, right_in),
                (right_mask_ref, right_mask),
                (left_ref, left_in),
                (left_mask_ref, left_mask),
                (prune_mask_ref, prune_mask),
            )
        )
    ]
    for fetch in fetches:
        fetch.start()

    own_slice = pl.ds(pl.multiple_of(l * deep, deep), deep)
    fetches[0].wait()
    fetches[1].wait()
    for h in range(2):
        for part in range(half // tile):
            mask = right_mask[0, 0, h * (half // tile) + part].astype(jnp.float32)
            block = right_in[:, h * half + part * tile : h * half + (part + 1) * tile]
            right_all[r, h, own_slice, part * tile : (part + 1) * tile] = (block.astype(jnp.float32) * mask).astype(
                jnp.bfloat16
            )
    def mask_left():
        fetches[2].wait()
        fetches[3].wait()
        for tall in range(2):
            for wide in range(2):
                mask = left_mask[tall, 0, wide].astype(jnp.float32)
                block = left_in[tall * tile : (tall + 1) * tile, wide * tile : (wide + 1) * tile]
                left_all[2 * c + wide, l, tall * tile : (tall + 1) * tile, :] = (
                    block.astype(jnp.float32) * mask
                ).astype(jnp.bfloat16)

    ways = (1, -1)

    def origin(way, step):
        return lax.rem(r - ways[way] * (step + 1) + 2 * nz, nz)

    def multiply(row, first=False):
        left = jnp.concatenate([left_all[row, 0], left_all[row, 1]], axis=1)
        product = jnp.dot(left, right_all[row, l], preferred_element_type=jnp.float32)
        if first:
            acc[...] = product
        else:
            acc[...] += product

    def multiply_step(step):
        for way in range(2):
            multiply(origin(way, step))

    right_swap_0 = send(right_all.at[r, :, pl.ds(0, deep)], swap_send.at[0], swap_recv.at[0], partner)
    right_swap_1 = send(right_all.at[r, 0, pl.ds(deep, deep)], swap_send.at[0], swap_recv.at[0], partner)
    left_swap_0 = send(left_all.at[pl.ds(2 * c, 2), 0], left_pass_send.at[0], left_pass_recv.at[0], partner)
    left_swap_1 = send(left_all.at[pl.ds(2 * c, 2), 1], swap_send.at[1], swap_recv.at[1], partner)
    steps = nz // 2

    def pass_group(step):
        if isinstance(step, int) and step >= steps - 2:
            return (steps - 2 + 3) // 4 + step - (steps - 2)
        return step // 4

    @pl.when(l == 1)
    def _():
        pl.semaphore_wait(barrier, 1 + len(ring_greeted))
        kinds = tuple((s, h, part) for s in (1, 0) for h in (0, 1) for part in range(PARTS))
        hops = ((steps - 1, steps), (steps, steps - 1))

        def block(kind, row):
            s, h, part = kinds[kind]
            return right_all.at[row, h, pl.ds(s * deep + part * (deep // PARTS), deep // PARTS)]

        def ring_copy(way, kind, step, row):
            s, h, _ = kinds[kind]
            recv_sem, device = ring_recv.at[way, kind, lax.rem(step, SLOTS)], at_z(ways[way])
            if isinstance(step, int) and final(way, kind, step):
                recv_sem, device = pass_recv.at[pass_group(step)], (device[0], c, 0)
            return send(block(kind, row), ring_send.at[0], recv_sem, device)

        def final(way, kind, step):
            s, h, _ = kinds[kind]
            return h == 0 and step == hops[s][way] - 1

        for kind in range(2 * PARTS):
            for way in range(2):
                ring_copy(way, kind, 0, r).start()
        right_swap_1.start()
        mask_left()
        left_swap_1.start()
        right_swap_0.wait_recv()
        for kind in range(2 * PARTS, 4 * PARTS):
            for way in range(2):
                ring_copy(way, kind, 0, r).start()

        def ring_step(step):
            last = isinstance(step, int)
            for kind, (s, h, _) in enumerate(kinds):
                for way in range(2):
                    if last and (step >= hops[s][way] or final(way, kind, step)):
                        continue
                    row = origin(way, step)
                    ring_copy(way, kind, step, row).wait_recv()
                    if not last or step + 1 < hops[s][way]:
                        ring_copy(way, kind, step + 1, row).start()
                    if h == 0:
                        send(block(kind, row), pass_send.at[0], pass_recv.at[pass_group(step)], partner).start()

        begin = BEGIN
        end = steps - 3
        each = -(-(steps - 1) // (steps - 1 - begin))
        lax.fori_loop(0, begin, lambda step, _: (ring_step(step), None)[1], None)
        send(left_all.at[pl.ds(0, nz - 1)], left_pass_send.at[0], left_pass_recv.at[0], partner).wait_recv()
        multiply(r, first=True)

        def both(step, _):
            ring_step(step)
            for turn in range(each):
                multiply_step(each * (step - begin) + turn)

        lax.fori_loop(begin, end, both, None)
        done = each * (end - begin)
        for step in range(end, steps - 1):
            ring_step(step)
            until = min(done + each, step + 1) if step < steps - 2 else step + 1
            for turn in range(done, until):
                multiply_step(turn)
            done = until
        ring_step(steps - 1)

    @pl.when(l == 0)
    def _():
        pl.semaphore_wait(barrier, 1 + len(left_greeted))
        right_swap_0.start()
        mask_left()
        left_swap_0.start()
        left_swap_1.wait_recv()
        peers = (at_x, at_y)

        def place(way, back, step=0):
            to_x, to_y = (back, step) if way == 0 else (step, back)
            return 2 * (lax.rem(y + SIDE - to_y, SIDE) * SIDE + lax.rem(x + SIDE - to_x, SIDE)) + way

        def first_copy(way, step, chunk):
            return send(left_all.at[chunk], left_send.at[0], first_recv.at[way, step - 1], peers[way](step))

        def second_copy(way, back, step, chunk):
            return send(left_all.at[chunk], left_send.at[0], second_recv.at[way, back], peers[1 - way](step))

        def pass_on(chunk):
            send(left_all.at[chunk], left_pass_send.at[0], left_pass_recv.at[0], partner).start()

        for step in range(1, SIDE):
            for way in range(2):
                first_copy(way, step, place(way, 0)).start()
        for step in range(1, SIDE):
            for way in range(2):
                second_copy(way, 0, step, place(way, 0)).start()
        for back in (1, 3, 2):
            for way in range(2):
                chunk = place(way, back)
                first_copy(way, back, chunk).wait_recv()
                for step in range(1, SIDE):
                    second_copy(way, back, step, chunk).start()
                pass_on(chunk)
        for back in (0, 1, 3, 2):
            for way in range(2):
                three = left_all.at[pl.ds(0, SIDE - 1)]
                send(three, left_send.at[0], second_recv.at[way, back], partner).wait_recv()
                for step in range(1, SIDE):
                    pass_on(place(way, back, step))

        right_swap_1.wait_recv()
        multiply(r, first=True)

        def received(group, count):
            send(right_all.at[pl.ds(0, count)], pass_send.at[0], pass_recv.at[group], partner).wait_recv()

        begun = 0
        while begun < steps - 2:
            count = min(4, steps - 2 - begun)
            received(pass_group(begun), count)
            lax.fori_loop(begun, begun + count, lambda step, _: (multiply_step(step), None)[1], None)
            begun += count
        received(pass_group(steps - 2), 1)
        multiply_step(steps - 2)
        send(right_all.at[0, 0], pass_send.at[0], pass_recv.at[pass_group(steps - 1)], partner).wait_recv()

    fetches[4].wait()
    rows = acc.shape[0]
    column_sum = None
    row = origin(0, steps - 1)
    left = jnp.concatenate([left_all[row, 0], left_all[row, 1]], axis=1)
    product = acc[...] + jnp.dot(left, right_all[row, l], preferred_element_type=jnp.float32)
    for tall in range(2):
        parts = []
        for wide in range(2):
            span = (slice(tall * tile, (tall + 1) * tile), slice(wide * tile, (wide + 1) * tile))
            value = product[span] * product[span] * prune_mask[tall, wide].astype(jnp.float32)
            acc[span] = value
            parts.append(jnp.sum(value, axis=0, keepdims=True))
        part = jnp.concatenate(parts, axis=1)
        column_sum = part if column_sum is None else column_sum + part
    own_sum[0] = column_sum

    far_first = [steps]
    for step in range(steps - 1, 0, -1):
        far_first += [step, nz - step]
    for index, step in enumerate(far_first):
        pltpu.make_async_remote_copy(
            src_ref=own_sum.at[0],
            dst_ref=sums.at[index],
            send_sem=sum_sem.at[0],
            recv_sem=sum_sem.at[1],
            device_id=at_z(step),
            device_id_type=MESH,
        ).start()

    @pl.when(l == 1)
    def _():
        right_swap_1.wait_send()
        left_swap_1.wait_send()
        send(right_all.at[pl.ds(0, nz - 1)], ring_send.at[0], ring_recv.at[0, 0, 0], partner).wait_send()
        send(right_all.at[pl.ds(0, nz - 3), 0], pass_send.at[0], pass_recv.at[0], partner).wait_send()

    @pl.when(l == 0)
    def _():
        right_swap_0.wait_send()
        send(left_all.at[pl.ds(0, nz - 2)], left_send.at[0], left_pass_recv.at[0], partner).wait_send()
        send(left_all.at[pl.ds(0, nz - 1)], left_pass_send.at[0], left_pass_recv.at[0], partner).wait_send()

    every = send(sums, sum_sem.at[0], sum_sem.at[1], partner)
    every.wait_recv()
    total = own_sum[0]
    for index in range(nz - 1):
        total += sums[index]
    out_ref[...] = acc[...] * ((rows * nz) / (total + epsilon))
    every.wait_send()


def on_device(nz, left_blocks, batch_blocks, left_mask, batch_mask, prune_mask):
    rows, _, depth = left_blocks.shape
    _, inner, columns = batch_blocks.shape
    tile = rows // left_mask.shape[0]
    half = columns // 2
    left = left_blocks.reshape(rows, depth)
    right = batch_blocks.reshape(inner, columns)
    dma = pltpu.SemaphoreType.DMA
    hbm = pl.BlockSpec(memory_space=pl.ANY)
    groups = (nz // 2 - 2 + 3) // 4 + 2
    return pl.pallas_call(
        functools.partial(kernel, nz),
        out_shape=pltpu.VMEM((rows, half), jnp.float32),
        in_specs=[hbm] * 5,
        out_specs=pl.BlockSpec(memory_space=pltpu.VMEM),
        scratch_shapes=[
            pltpu.VMEM((rows, depth), jnp.bfloat16),
            pltpu.VMEM((inner, columns), jnp.bfloat16),
            pltpu.SMEM(left_mask.shape, jnp.int32),
            pltpu.SMEM(batch_mask.shape, jnp.int32),
            pltpu.SMEM(prune_mask.shape, jnp.int32),
            pltpu.VMEM((nz, 2, rows, tile), jnp.bfloat16),
            pltpu.VMEM((nz, 2, 2 * inner, half), jnp.bfloat16),
            pltpu.VMEM((rows, half), jnp.float32),
            pltpu.VMEM((1, 1, half), jnp.float32),
            pltpu.VMEM((nz - 1, 1, half), jnp.float32),
            dma((5,)),
            dma((2,)),
            dma((2,)),
            dma((1,)),
            dma((2, 4 * PARTS, SLOTS)),
            dma((1,)),
            dma((groups,)),
            dma((1,)),
            dma((2, SIDE - 1)),
            dma((2, SIDE)),
            dma((1,)),
            dma((1,)),
            dma((2,)),
        ],
        compiler_params=pltpu.CompilerParams(collective_id=0, has_side_effects=True),
    )(left, right, left_mask, batch_mask, prune_mask)


def solution(mesh):
    placed = (
        P("row", "layer", "col"),
        P("layer", "row", "col"),
        P("row", "layer", "col"),
        P("layer", "row", "col"),
        P("row", ("col", "layer")),
    )
    return jax.shard_map(
        functools.partial(on_device, mesh.shape["row"]),
        mesh=mesh,
        in_specs=placed,
        out_specs=P("row", ("col", "layer")),
        check_vma=False,
    )
```

```python
import functools

import jax
import jax.numpy as jnp
from jax import lax
from jax.experimental import pallas as pl
from jax.experimental.pallas import tpu as pltpu
from jax.sharding import PartitionSpec as P

epsilon = 1e-06
MESH = pl.DeviceIdType.MESH
SIDE = 4
PARTS = 2
SLOTS = 3
BEGIN = 9


def kernel(
    nz,
    left_ref,
    right_ref,
    left_mask_ref,
    right_mask_ref,
    prune_mask_ref,
    out_ref,
    left_in,
    right_in,
    left_mask,
    right_mask,
    prune_mask,
    left_all,
    right_all,
    acc,
    own_sum,
    sums,
    in_sem,
    swap_send,
    swap_recv,
    ring_send,
    ring_recv,
    pass_send,
    pass_recv,
    left_send,
    first_recv,
    second_recv,
    left_pass_send,
    left_pass_recv,
    sum_sem,
):
    r = lax.axis_index("row")
    c = lax.axis_index("col")
    l = lax.axis_index("layer")
    y, x = c // SIDE, c % SIDE
    deep = left_all.shape[3]
    tile = deep
    half = right_all.shape[3]

    def at_z(step):
        return (lax.rem(r + step + nz, nz), c, l)

    def at_x(step):
        return (r, y * SIDE + lax.rem(x + step + SIDE, SIDE), l)

    def at_y(step):
        return (r, lax.rem(y + step + SIDE, SIDE) * SIDE + x, l)

    partner = (r, c, 1 - l)

    def send(block, send_sem, recv_sem, device):
        return pltpu.make_async_remote_copy(
            src_ref=block,
            dst_ref=block,
            send_sem=send_sem,
            recv_sem=recv_sem,
            device_id=device,
            device_id_type=MESH,
        )

    barrier = pltpu.get_barrier_semaphore()

    def greet(devices):
        for device in devices:
            pl.semaphore_signal(barrier, inc=1, device_id=device, device_id_type=MESH)

    heard = (2, 7)
    pl.when(l == 1)(lambda: greet([at_z(1), at_z(-1), (at_z(1)[0], c, 0), (at_z(-1)[0], c, 0), partner]))
    pl.when(l == 0)(lambda: greet([at_x(1), at_x(-1), at_y(1), at_y(-1)]))

    fetches = [
        pltpu.make_async_copy(source, target, in_sem.at[index])
        for index, (source, target) in enumerate(
            (
                (right_ref, right_in),
                (right_mask_ref, right_mask),
                (left_ref, left_in),
                (left_mask_ref, left_mask),
                (prune_mask_ref, prune_mask),
            )
        )
    ]
    for fetch in fetches:
        fetch.start()

    own_slice = pl.ds(pl.multiple_of(l * deep, deep), deep)
    fetches[0].wait()
    fetches[1].wait()
    for h in range(2):
        for part in range(half // tile):
            mask = right_mask[0, 0, h * (half // tile) + part].astype(jnp.float32)
            block = right_in[:, h * half + part * tile : h * half + (part + 1) * tile]
            right_all[r, h, own_slice, part * tile : (part + 1) * tile] = (block.astype(jnp.float32) * mask).astype(
                jnp.bfloat16
            )

    def mask_left():
        fetches[2].wait()
        fetches[3].wait()
        for tall in range(2):
            for wide in range(2):
                mask = left_mask[tall, 0, wide].astype(jnp.float32)
                block = left_in[tall * tile : (tall + 1) * tile, wide * tile : (wide + 1) * tile]
                left_all[2 * c + wide, l, tall * tile : (tall + 1) * tile, :] = (
                    block.astype(jnp.float32) * mask
                ).astype(jnp.bfloat16)

    ways = (1, -1)

    def origin(way, step):
        return lax.rem(r - ways[way] * (step + 1) + 2 * nz, nz)

    def multiply(row, first=False):
        left = jnp.concatenate([left_all[row, 0], left_all[row, 1]], axis=1)
        product = jnp.dot(left, right_all[row, l], preferred_element_type=jnp.float32)
        if first:
            acc[...] = product
        else:
            acc[...] += product

    def multiply_step(step):
        for way in range(2):
            multiply(origin(way, step))

    right_swap_0 = send(right_all.at[r, :, pl.ds(0, deep)], swap_send.at[0], swap_recv.at[0], partner)
    right_swap_1 = send(right_all.at[r, 0, pl.ds(deep, deep)], swap_send.at[0], swap_recv.at[0], partner)
    left_swap_0 = send(left_all.at[pl.ds(2 * c, 2), 0], left_pass_send.at[0], left_pass_recv.at[0], partner)
    left_swap_1 = send(left_all.at[pl.ds(2 * c, 2), 1], swap_send.at[1], swap_recv.at[1], partner)
    steps = nz // 2

    def pass_group(step):
        if isinstance(step, int) and step >= steps - 2:
            return (steps - 2 + 3) // 4 + step - (steps - 2)
        return step // 4

    kinds = tuple((s, h, part) for s in (1, 0) for h in (0, 1) for part in range(PARTS))
    hops = ((steps - 1, steps), (steps, steps - 1))

    def block(kind, row):
        s, h, part = kinds[kind]
        return right_all.at[row, h, pl.ds(s * deep + part * (deep // PARTS), deep // PARTS)]

    def ring_copy(way, kind, step, row, core=None):
        s, h, _ = kinds[kind]
        recv_sem, device = ring_recv.at[way, kind, lax.rem(step, SLOTS)], at_z(ways[way])
        if core is not None:
            device = (device[0], c, core)
        if isinstance(step, int) and final(way, kind, step):
            recv_sem, device = pass_recv.at[pass_group(step)], (device[0], c, 0)
        return send(block(kind, row), ring_send.at[0], recv_sem, device)

    def final(way, kind, step):
        s, h, _ = kinds[kind]
        return h == 0 and step == hops[s][way] - 1

    @pl.when(l == 1)
    def _():
        pl.semaphore_wait(barrier, heard[0])
        for kind in range(2 * PARTS):
            for way in range(2):
                ring_copy(way, kind, 0, r).start()
        mask_left()
        right_swap_0.wait_recv()
        right_swap_1.start()
        left_swap_1.start()

        def ring_step(step):
            last = isinstance(step, int)
            for kind, (s, h, _) in enumerate(kinds):
                for way in range(2):
                    if last and (step >= hops[s][way] or final(way, kind, step)):
                        continue
                    row = origin(way, step)
                    ring_copy(way, kind, step, row).wait_recv()
                    if not last or step + 1 < hops[s][way]:
                        ring_copy(way, kind, step + 1, row).start()
                    if h == 0:
                        send(block(kind, row), pass_send.at[0], pass_recv.at[pass_group(step)], partner).start()

        begin = BEGIN
        end = steps - 3
        each = -(-(steps - 1) // (steps - 1 - begin))
        lax.fori_loop(0, begin, lambda step, _: (ring_step(step), None)[1], None)
        send(left_all.at[pl.ds(0, nz - 1)], left_pass_send.at[0], left_pass_recv.at[0], partner).wait_recv()
        multiply(r, first=True)

        def both(step, _):
            ring_step(step)
            for turn in range(each):
                multiply_step(each * (step - begin) + turn)

        lax.fori_loop(begin, end, both, None)
        done = each * (end - begin)
        for step in range(end, steps - 1):
            ring_step(step)
            until = min(done + each, step + 1) if step < steps - 2 else step + 1
            for turn in range(done, until):
                multiply_step(turn)
            done = until
        ring_step(steps - 1)

    @pl.when(l == 0)
    def _():
        pl.semaphore_wait(barrier, heard[1])
        for kind in range(2 * PARTS, 4 * PARTS):
            for way in range(2):
                ring_copy(way, kind, 0, r, core=1).start()
        right_swap_0.start()
        mask_left()
        left_swap_0.start()
        left_swap_1.wait_recv()
        peers = (at_x, at_y)

        def place(way, back, step=0):
            to_x, to_y = (back, step) if way == 0 else (step, back)
            return 2 * (lax.rem(y + SIDE - to_y, SIDE) * SIDE + lax.rem(x + SIDE - to_x, SIDE)) + way

        def first_copy(way, step, chunk):
            return send(left_all.at[chunk], left_send.at[0], first_recv.at[way, step - 1], peers[way](step))

        def second_copy(way, back, step, chunk):
            return send(left_all.at[chunk], left_send.at[0], second_recv.at[way, back], peers[1 - way](step))

        def pass_on(chunk):
            send(left_all.at[chunk], left_pass_send.at[0], left_pass_recv.at[0], partner).start()

        near = (1, SIDE - 1)
        for copy in (first_copy, functools.partial(second_copy, back=0)):
            for step in near:
                for way in range(2):
                    copy(way, step=step, chunk=place(way, 0)).start()
        for way in range(2):
            first_copy(way, 1, place(way, 1)).wait_recv()
        for copy in (first_copy, functools.partial(second_copy, back=0)):
            for step in range(2, SIDE - 1):
                for way in range(2):
                    copy(way, step=step, chunk=place(way, 0)).start()
        for back in (1, 3, 2):
            for way in range(2):
                chunk = place(way, back)
                if back != 1:
                    first_copy(way, back, chunk).wait_recv()
                for step in range(1, SIDE):
                    second_copy(way, back, step, chunk).start()
                pass_on(chunk)
        for back in (0, 1, 3, 2):
            for way in range(2):
                three = left_all.at[pl.ds(0, SIDE - 1)]
                send(three, left_send.at[0], second_recv.at[way, back], partner).wait_recv()
                for step in range(1, SIDE):
                    pass_on(place(way, back, step))

        right_swap_1.wait_recv()
        multiply(r, first=True)

        def received(group, count):
            send(right_all.at[pl.ds(0, count)], pass_send.at[0], pass_recv.at[group], partner).wait_recv()

        begun = 0
        while begun < steps - 2:
            count = min(4, steps - 2 - begun)
            received(pass_group(begun), count)
            lax.fori_loop(begun, begun + count, lambda step, _: (multiply_step(step), None)[1], None)
            begun += count
        received(pass_group(steps - 2), 1)
        multiply_step(steps - 2)
        send(right_all.at[0, 0], pass_send.at[0], pass_recv.at[pass_group(steps - 1)], partner).wait_recv()

    fetches[4].wait()
    rows = acc.shape[0]
    column_sum = None
    row = origin(0, steps - 1)
    left = jnp.concatenate([left_all[row, 0], left_all[row, 1]], axis=1)
    product = acc[...] + jnp.dot(left, right_all[row, l], preferred_element_type=jnp.float32)
    for tall in range(2):
        parts = []
        for wide in range(2):
            span = (slice(tall * tile, (tall + 1) * tile), slice(wide * tile, (wide + 1) * tile))
            value = product[span] * product[span] * prune_mask[tall, wide].astype(jnp.float32)
            acc[span] = value
            parts.append(jnp.sum(value, axis=0, keepdims=True))
        part = jnp.concatenate(parts, axis=1)
        column_sum = part if column_sum is None else column_sum + part
    own_sum[0] = column_sum

    far_first = [steps]
    for step in range(steps - 1, 0, -1):
        far_first += [step, nz - step]
    for index, step in enumerate(far_first):
        pltpu.make_async_remote_copy(
            src_ref=own_sum.at[0],
            dst_ref=sums.at[index],
            send_sem=sum_sem.at[0],
            recv_sem=sum_sem.at[1],
            device_id=at_z(step),
            device_id_type=MESH,
        ).start()

    @pl.when(l == 1)
    def _():
        right_swap_1.wait_send()
        left_swap_1.wait_send()
        send(right_all.at[pl.ds(0, nz - 2)], ring_send.at[0], ring_recv.at[0, 0, 0], partner).wait_send()
        send(right_all.at[pl.ds(0, nz - 3), 0], pass_send.at[0], pass_recv.at[0], partner).wait_send()

    @pl.when(l == 0)
    def _():
        right_swap_0.wait_send()
        send(right_all.at[0], ring_send.at[0], ring_recv.at[0, 0, 0], partner).wait_send()
        send(left_all.at[pl.ds(0, nz - 2)], left_send.at[0], left_pass_recv.at[0], partner).wait_send()
        send(left_all.at[pl.ds(0, nz - 1)], left_pass_send.at[0], left_pass_recv.at[0], partner).wait_send()

    every = send(sums, sum_sem.at[0], sum_sem.at[1], partner)
    every.wait_recv()
    total = own_sum[0]
    for index in range(nz - 1):
        total += sums[index]
    out_ref[...] = acc[...] * ((rows * nz) / (total + epsilon))
    every.wait_send()


def on_device(nz, left_blocks, batch_blocks, left_mask, batch_mask, prune_mask):
    rows, _, depth = left_blocks.shape
    _, inner, columns = batch_blocks.shape
    tile = rows // left_mask.shape[0]
    half = columns // 2
    left = left_blocks.reshape(rows, depth)
    right = batch_blocks.reshape(inner, columns)
    dma = pltpu.SemaphoreType.DMA
    hbm = pl.BlockSpec(memory_space=pl.ANY)
    groups = (nz // 2 - 2 + 3) // 4 + 2
    return pl.pallas_call(
        functools.partial(kernel, nz),
        out_shape=pltpu.VMEM((rows, half), jnp.float32),
        in_specs=[hbm] * 5,
        out_specs=pl.BlockSpec(memory_space=pltpu.VMEM),
        scratch_shapes=[
            pltpu.VMEM((rows, depth), jnp.bfloat16),
            pltpu.VMEM((inner, columns), jnp.bfloat16),
            pltpu.SMEM(left_mask.shape, jnp.int32),
            pltpu.SMEM(batch_mask.shape, jnp.int32),
            pltpu.SMEM(prune_mask.shape, jnp.int32),
            pltpu.VMEM((nz, 2, rows, tile), jnp.bfloat16),
            pltpu.VMEM((nz, 2, 2 * inner, half), jnp.bfloat16),
            pltpu.VMEM((rows, half), jnp.float32),
            pltpu.VMEM((1, 1, half), jnp.float32),
            pltpu.VMEM((nz - 1, 1, half), jnp.float32),
            dma((5,)),
            dma((2,)),
            dma((2,)),
            dma((1,)),
            dma((2, 4 * PARTS, SLOTS)),
            dma((1,)),
            dma((groups,)),
            dma((1,)),
            dma((2, SIDE - 1)),
            dma((2, SIDE)),
            dma((1,)),
            dma((1,)),
            dma((2,)),
        ],
        compiler_params=pltpu.CompilerParams(collective_id=0, has_side_effects=True),
    )(left, right, left_mask, batch_mask, prune_mask)


def solution(mesh):
    placed = (
        P("row", "layer", "col"),
        P("layer", "row", "col"),
        P("row", "layer", "col"),
        P("layer", "row", "col"),
        P("row", ("col", "layer")),
    )
    return jax.shard_map(
        functools.partial(on_device, mesh.shape["row"]),
        mesh=mesh,
        in_specs=placed,
        out_specs=P("row", ("col", "layer")),
        check_vma=False,
    )
```

```python
import functools

import jax
import jax.numpy as jnp
from jax import lax
from jax.experimental import pallas as pl
from jax.experimental.pallas import tpu as pltpu
from jax.sharding import PartitionSpec as P

epsilon = 1e-06
MESH = pl.DeviceIdType.MESH
SIDE = 4
PARTS = 2
SLOTS = 3
BEGIN = 10


def kernel(
    nz,
    left_ref,
    right_ref,
    left_mask_ref,
    right_mask_ref,
    prune_mask_ref,
    out_ref,
    left_in,
    right_in,
    left_mask,
    right_mask,
    prune_mask,
    left_all,
    right_all,
    acc,
    own_sum,
    sums,
    in_sem,
    swap_send,
    swap_recv,
    ring_send,
    ring_recv,
    pass_send,
    pass_recv,
    left_send,
    first_recv,
    second_recv,
    left_pass_send,
    left_pass_recv,
    sum_sem,
):
    r = lax.axis_index("row")
    c = lax.axis_index("col")
    l = lax.axis_index("layer")
    y, x = c // SIDE, c % SIDE
    deep = left_all.shape[3]
    tile = deep
    half = right_all.shape[3]

    def at_z(step):
        return (lax.rem(r + step + nz, nz), c, l)

    def at_x(step):
        return (r, y * SIDE + lax.rem(x + step + SIDE, SIDE), l)

    def at_y(step):
        return (r, lax.rem(y + step + SIDE, SIDE) * SIDE + x, l)

    partner = (r, c, 1 - l)

    def send(block, send_sem, recv_sem, device):
        return pltpu.make_async_remote_copy(
            src_ref=block,
            dst_ref=block,
            send_sem=send_sem,
            recv_sem=recv_sem,
            device_id=device,
            device_id_type=MESH,
        )

    barrier = pltpu.get_barrier_semaphore()

    def greet(devices):
        for device in devices:
            pl.semaphore_signal(barrier, inc=1, device_id=device, device_id_type=MESH)

    heard = (2, 7)
    pl.when(l == 1)(lambda: greet([at_z(1), at_z(-1), (at_z(1)[0], c, 0), (at_z(-1)[0], c, 0), partner]))
    pl.when(l == 0)(lambda: greet([at_x(1), at_x(-1), at_y(1), at_y(-1)]))

    fetches = [
        pltpu.make_async_copy(source, target, in_sem.at[index])
        for index, (source, target) in enumerate(
            (
                (right_ref, right_in),
                (right_mask_ref, right_mask),
                (left_ref, left_in),
                (left_mask_ref, left_mask),
                (prune_mask_ref, prune_mask),
            )
        )
    ]
    for fetch in fetches:
        fetch.start()

    own_slice = pl.ds(pl.multiple_of(l * deep, deep), deep)
    fetches[0].wait()
    fetches[1].wait()
    for h in range(2):
        for part in range(half // tile):
            mask = right_mask[0, 0, h * (half // tile) + part].astype(jnp.float32)
            block = right_in[:, h * half + part * tile : h * half + (part + 1) * tile]
            right_all[r, h, own_slice, part * tile : (part + 1) * tile] = (block.astype(jnp.float32) * mask).astype(
                jnp.bfloat16
            )

    def mask_left():
        fetches[2].wait()
        fetches[3].wait()
        for tall in range(2):
            for wide in range(2):
                mask = left_mask[tall, 0, wide].astype(jnp.float32)
                block = left_in[tall * tile : (tall + 1) * tile, wide * tile : (wide + 1) * tile]
                left_all[2 * c + wide, l, tall * tile : (tall + 1) * tile, :] = (
                    block.astype(jnp.float32) * mask
                ).astype(jnp.bfloat16)

    ways = (1, -1)

    def origin(way, step):
        return lax.rem(r - ways[way] * (step + 1) + 2 * nz, nz)

    def multiply(row, first=False):
        left = jnp.concatenate([left_all[row, 0], left_all[row, 1]], axis=1)
        product = jnp.dot(left, right_all[row, l], preferred_element_type=jnp.float32)
        if first:
            acc[...] = product
        else:
            acc[...] += product

    def multiply_step(step):
        for way in range(2):
            multiply(origin(way, step))

    right_swap_0 = send(right_all.at[r, :, pl.ds(0, deep)], swap_send.at[0], swap_recv.at[0], partner)
    right_swap_1 = send(right_all.at[r, 0, pl.ds(deep, deep)], swap_send.at[0], swap_recv.at[0], partner)
    left_swap_0 = send(left_all.at[pl.ds(2 * c, 2), 0], left_pass_send.at[0], left_pass_recv.at[0], partner)
    left_swap_1 = send(left_all.at[pl.ds(2 * c, 2), 1], swap_send.at[1], swap_recv.at[1], partner)
    steps = nz // 2

    def pass_group(step):
        if isinstance(step, int) and step >= steps - 2:
            return (steps - 2 + 3) // 4 + step - (steps - 2)
        return step // 4

    kinds = tuple((s, h, part) for s in (1, 0) for h in (0, 1) for part in range(PARTS))
    hops = ((steps - 1, steps), (steps, steps - 1))

    def block(kind, row):
        s, h, part = kinds[kind]
        return right_all.at[row, h, pl.ds(s * deep + part * (deep // PARTS), deep // PARTS)]

    def ring_copy(way, kind, step, row, core=None):
        s, h, _ = kinds[kind]
        recv_sem, device = ring_recv.at[way, kind, lax.rem(step, SLOTS)], at_z(ways[way])
        if core is not None:
            device = (device[0], c, core)
        if isinstance(step, int) and final(way, kind, step):
            recv_sem, device = pass_recv.at[pass_group(step)], (device[0], c, 0)
        return send(block(kind, row), ring_send.at[0], recv_sem, device)

    def final(way, kind, step):
        s, h, _ = kinds[kind]
        return h == 0 and step == hops[s][way] - 1

    @pl.when(l == 1)
    def _():
        pl.semaphore_wait(barrier, heard[0])
        for kind in range(2 * PARTS):
            for way in range(2):
                ring_copy(way, kind, 0, r).start()
        mask_left()
        right_swap_0.wait_recv()
        right_swap_1.start()
        left_swap_1.start()

        def ring_step(step):
            last = isinstance(step, int)
            for kind, (s, h, _) in enumerate(kinds):
                for way in range(2):
                    if last and (step >= hops[s][way] or final(way, kind, step)):
                        continue
                    row = origin(way, step)
                    ring_copy(way, kind, step, row).wait_recv()
                    if not last or step + 1 < hops[s][way]:
                        ring_copy(way, kind, step + 1, row).start()
                    if h == 0:
                        send(block(kind, row), pass_send.at[0], pass_recv.at[pass_group(step)], partner).start()

        begin = BEGIN
        end = steps - 3
        each = -(-(steps - 1) // (steps - 1 - begin))
        lax.fori_loop(0, begin, lambda step, _: (ring_step(step), None)[1], None)
        send(left_all.at[pl.ds(0, nz - 1)], left_pass_send.at[0], left_pass_recv.at[0], partner).wait_recv()
        multiply(r, first=True)

        def both(step, _):
            ring_step(step)
            for turn in range(each):
                multiply_step(each * (step - begin) + turn)

        lax.fori_loop(begin, end, both, None)
        done = each * (end - begin)
        for step in range(end, steps - 1):
            ring_step(step)
            until = min(done + each, step + 1) if step < steps - 2 else step + 1
            for turn in range(done, until):
                multiply_step(turn)
            done = until
        ring_step(steps - 1)

    @pl.when(l == 0)
    def _():
        pl.semaphore_wait(barrier, heard[1])
        for kind in range(2 * PARTS, 4 * PARTS):
            for way in range(2):
                ring_copy(way, kind, 0, r, core=1).start()
        right_swap_0.start()
        mask_left()
        left_swap_0.start()
        left_swap_1.wait_recv()
        peers = (at_x, at_y)

        def place(way, back, step=0):
            to_x, to_y = (back, step) if way == 0 else (step, back)
            return 2 * (lax.rem(y + SIDE - to_y, SIDE) * SIDE + lax.rem(x + SIDE - to_x, SIDE)) + way

        def first_copy(way, step, chunk):
            return send(left_all.at[chunk], left_send.at[0], first_recv.at[way, step - 1], peers[way](step))

        def second_copy(way, back, step, chunk):
            return send(left_all.at[chunk], left_send.at[0], second_recv.at[way, back], peers[1 - way](step))

        def pass_on(chunk):
            send(left_all.at[chunk], left_pass_send.at[0], left_pass_recv.at[0], partner).start()

        near = (1, SIDE - 1)
        for copy in (first_copy, functools.partial(second_copy, back=0)):
            for step in near:
                for way in range(2):
                    copy(way, step=step, chunk=place(way, 0)).start()
        for way in range(2):
            first_copy(way, 1, place(way, 1)).wait_recv()
        for copy in (first_copy, functools.partial(second_copy, back=0)):
            for step in range(2, SIDE - 1):
                for way in range(2):
                    copy(way, step=step, chunk=place(way, 0)).start()
        for back in (1, 3, 2):
            for way in range(2):
                chunk = place(way, back)
                if back != 1:
                    first_copy(way, back, chunk).wait_recv()
                for step in range(1, SIDE):
                    second_copy(way, back, step, chunk).start()
                pass_on(chunk)
        for back in (0, 1, 3, 2):
            for way in range(2):
                three = left_all.at[pl.ds(0, SIDE - 1)]
                send(three, left_send.at[0], second_recv.at[way, back], partner).wait_recv()
                for step in range(1, SIDE):
                    pass_on(place(way, back, step))

        right_swap_1.wait_recv()
        multiply(r, first=True)

        def received(group, count):
            send(right_all.at[pl.ds(0, count)], pass_send.at[0], pass_recv.at[group], partner).wait_recv()

        begun = 0
        while begun < steps - 2:
            count = min(4, steps - 2 - begun)
            received(pass_group(begun), count)
            lax.fori_loop(begun, begun + count, lambda step, _: (multiply_step(step), None)[1], None)
            begun += count
        received(pass_group(steps - 2), 1)
        multiply_step(steps - 2)
        send(right_all.at[0, 0], pass_send.at[0], pass_recv.at[pass_group(steps - 1)], partner).wait_recv()

    fetches[4].wait()
    rows = acc.shape[0]
    column_sum = None
    row = origin(0, steps - 1)
    left = jnp.concatenate([left_all[row, 0], left_all[row, 1]], axis=1)
    product = acc[...] + jnp.dot(left, right_all[row, l], preferred_element_type=jnp.float32)
    for tall in range(2):
        parts = []
        for wide in range(2):
            span = (slice(tall * tile, (tall + 1) * tile), slice(wide * tile, (wide + 1) * tile))
            value = product[span] * product[span] * prune_mask[tall, wide].astype(jnp.float32)
            acc[span] = value
            parts.append(jnp.sum(value, axis=0, keepdims=True))
        part = jnp.concatenate(parts, axis=1)
        column_sum = part if column_sum is None else column_sum + part
    own_sum[0] = column_sum

    far_first = [steps]
    for step in range(steps - 1, 0, -1):
        far_first += [step, nz - step]
    for index, step in enumerate(far_first):
        pltpu.make_async_remote_copy(
            src_ref=own_sum.at[0],
            dst_ref=sums.at[index],
            send_sem=sum_sem.at[0],
            recv_sem=sum_sem.at[1],
            device_id=at_z(step),
            device_id_type=MESH,
        ).start()

    @pl.when(l == 1)
    def _():
        right_swap_1.wait_send()
        left_swap_1.wait_send()
        send(right_all.at[pl.ds(0, nz - 2)], ring_send.at[0], ring_recv.at[0, 0, 0], partner).wait_send()
        send(right_all.at[pl.ds(0, nz - 3), 0], pass_send.at[0], pass_recv.at[0], partner).wait_send()

    @pl.when(l == 0)
    def _():
        right_swap_0.wait_send()
        send(right_all.at[0], ring_send.at[0], ring_recv.at[0, 0, 0], partner).wait_send()
        send(left_all.at[pl.ds(0, nz - 2)], left_send.at[0], left_pass_recv.at[0], partner).wait_send()
        send(left_all.at[pl.ds(0, nz - 1)], left_pass_send.at[0], left_pass_recv.at[0], partner).wait_send()

    every = send(sums, sum_sem.at[0], sum_sem.at[1], partner)
    every.wait_recv()
    total = own_sum[0]
    for index in range(nz - 1):
        total += sums[index]
    out_ref[...] = acc[...] * ((rows * nz) / (total + epsilon))
    every.wait_send()


def on_device(nz, left_blocks, batch_blocks, left_mask, batch_mask, prune_mask):
    rows, _, depth = left_blocks.shape
    _, inner, columns = batch_blocks.shape
    tile = rows // left_mask.shape[0]
    half = columns // 2
    left = left_blocks.reshape(rows, depth)
    right = batch_blocks.reshape(inner, columns)
    dma = pltpu.SemaphoreType.DMA
    hbm = pl.BlockSpec(memory_space=pl.ANY)
    groups = (nz // 2 - 2 + 3) // 4 + 2
    return pl.pallas_call(
        functools.partial(kernel, nz),
        out_shape=pltpu.VMEM((rows, half), jnp.float32),
        in_specs=[hbm] * 5,
        out_specs=pl.BlockSpec(memory_space=pltpu.VMEM),
        scratch_shapes=[
            pltpu.VMEM((rows, depth), jnp.bfloat16),
            pltpu.VMEM((inner, columns), jnp.bfloat16),
            pltpu.SMEM(left_mask.shape, jnp.int32),
            pltpu.SMEM(batch_mask.shape, jnp.int32),
            pltpu.SMEM(prune_mask.shape, jnp.int32),
            pltpu.VMEM((nz, 2, rows, tile), jnp.bfloat16),
            pltpu.VMEM((nz, 2, 2 * inner, half), jnp.bfloat16),
            pltpu.VMEM((rows, half), jnp.float32),
            pltpu.VMEM((1, 1, half), jnp.float32),
            pltpu.VMEM((nz - 1, 1, half), jnp.float32),
            dma((5,)),
            dma((2,)),
            dma((2,)),
            dma((1,)),
            dma((2, 4 * PARTS, SLOTS)),
            dma((1,)),
            dma((groups,)),
            dma((1,)),
            dma((2, SIDE - 1)),
            dma((2, SIDE)),
            dma((1,)),
            dma((1,)),
            dma((2,)),
        ],
        compiler_params=pltpu.CompilerParams(collective_id=0, has_side_effects=True),
    )(left, right, left_mask, batch_mask, prune_mask)


def solution(mesh):
    placed = (
        P("row", "layer", "col"),
        P("layer", "row", "col"),
        P("row", "layer", "col"),
        P("layer", "row", "col"),
        P("row", ("col", "layer")),
    )
    return jax.shard_map(
        functools.partial(on_device, mesh.shape["row"]),
        mesh=mesh,
        in_specs=placed,
        out_specs=P("row", ("col", "layer")),
        check_vma=False,
    )
```
